128 devices in a mesh: blk: 128 (over z, x, y, core).
Axes of the slice: x: 4, y: 4, z: 4, core: 2. Of those that a mesh axis runs over, the one named last changes fastest.
Arguments:
- state: float32 [4, 2048, 128, 256], P(None, 'blk'), may hold values from -6 to 6
- sample_cell: int32 [65536], P('blk'), may hold values from 0 to 491262, as said below
- sample_frac: float32 [3, 65536], P(None, 'blk'), may hold values from 0 to 1
- sample_owner: int32 [65536, 1], P('blk'), may hold values from 0 to 127; in each aligned block of 512 rows (0 to 511, 512 to 1023, ...) at most 8 rows name the same one
- face_angles: float32 [2, 131072], P(None, 'blk'), may hold values from -3.140625 to 3.140625
- face_height: float32 [131072], P('blk'), may hold values from 0.05 to 0.5
- wall_temp: float32 [131072], P('blk'), may hold values from -6 to 6
- face_visc: float32 [131072], P('blk'), may hold values from 0.005 to 0.05
Outputs:
- final_state: float32 [4, 2048, 128, 256], P(None, 'blk')
- wall_flux: float32 [4, 65536], P(None, 'blk')
The draws below stay inside these ranges and needn't reach their ends.
Inputs may be any that keep to these rules, and one draw needn't show every extreme that they name: `sample_cell`: index i * 128 * 256 + j * 256 + k with i < 15, j < 127, k < 255, so that the whole block lies in the partition. `sample_owner`: among the 512 exchange points of one partition no owner is named more than 8 times, a bound that some block reaches.
All inputs are finite; a program needn't handle non-finite values.
Results may differ from the reference program's by a relative error of at most 0.0003.
Values sent between devices are 32-bit elements; how exact they have to be, the bound alone decides.
No kernel may reach another device: no remote copies, remote signals or barrier semaphores. Data moves between devices by JAX's collectives and lax.ppermute only.
A program may use at most 128 MiB of HBM per device.

```python
import math
import jax
import jax.numpy as jnp
import numpy as np
from jax import lax

CX = 16
NY = 128
NZ = 256
EP_DEV = 512
NPTS = 64
NEWTON = 3
CAP = 8
NX = 2048
EXCH = 65536
FACE_SLOTS = 131072
N_BLK = 128


def draw_sample_cell(key, part):
    key_x, key_y, key_z = jax.random.split(key, 3)
    along_x = jax.random.randint(key_x, (EXCH,), 0, CX - 1)
    along_y = jax.random.randint(key_y, (EXCH,), 0, NY - 1)
    along_z = jax.random.randint(key_z, (EXCH,), 0, NZ - 1)
    cells = along_x * (NY * NZ) + along_y * NZ + along_z
    blocks = cells.reshape(EXCH // EP_DEV, EP_DEV)
    blocks = blocks.at[:, 0].set((CX - 2) * NY * NZ + (NY - 2) * NZ + NZ - 2)
    blocks = blocks.at[:, 1].set(0)
    return blocks.reshape(EXCH).astype(jnp.int32)


def shard_levels(rng, shape, pieces, low, high):
    def one(dim, shards_of):
        draws = jax.random.uniform(jax.random.fold_in(jax.random.fold_in(rng, 6), dim), (shards_of,), jnp.float32, low / len(pieces), high / len(pieces))
        return jnp.repeat(jnp.exp(draws), shape[dim] // shards_of).reshape((-1,) + (1,) * (len(shape) - dim - 1))

    factor_of = one(*pieces[0])
    for cut in pieces[1:]:
        factor_of = factor_of * one(*cut)
    return factor_of


def deal_out(own_key, own, number, rows, amount, top, most, lean):
    ranking = jax.random.permutation(own_key, amount)
    heavy_load, ordinary = load_shares(amount, rows * top, most, lean, True), load_shares(amount, rows * top, most, lean, False)
    places = jnp.arange(amount)

    def named(lengths, turn):
        used = int((lengths > 0).sum())
        fixed = max(1, used // 4)
        moved = fixed + (places - fixed + turn * (used - fixed)) % max(1, amount - fixed)
        return jnp.zeros((amount,), jnp.int32).at[ranking[jnp.where(places < fixed, places, moved)]].set(jnp.asarray(lengths, jnp.int32))

    lengths = jnp.where(number % 4 == 0, named(heavy_load, number // 4), named(ordinary, number - number // 4 - 1))
    mixed = jax.random.permutation(jax.random.fold_in(own, 3), amount)
    source_of, sink = mixed[0:amount // 2 * 2:2], mixed[1:amount // 2 * 2:2]
    room = jnp.minimum(lengths[source_of] - 1, most - lengths[sink]) // 2
    room = jnp.where((source_of == ranking[0]) | (sink == ranking[0]) | (lengths[sink] == 0), 0, jnp.maximum(room, 0))
    moved = jax.random.randint(jax.random.fold_in(own, 4), (amount // 2,), 0, 1 << 20) % (room + 1)
    lengths = lengths.at[source_of].add(-moved).at[sink].add(moved)
    items = jnp.searchsorted(jnp.cumsum(lengths), jnp.arange(rows * top), side="right").astype(jnp.int32)
    table = items.reshape(top, rows).T
    table = table[jax.random.permutation(jax.random.fold_in(own, 1), rows)]
    turn = jax.random.randint(jax.random.fold_in(own, 2), (rows, 1), 0, top)
    return jnp.take_along_axis(table, (jnp.arange(top)[None, :] + turn) % top, axis=1)


def load_shares(amount, total, limit, skew, full):
    loads = [(1 << 20) // math.isqrt(grade ** skew) + 1 for grade in range(1, amount + 1)]
    largest = limit if full else min(limit, max(-(-total // amount), total * loads[0] // sum(loads)))
    least = 1 if total - largest >= amount - 1 else 0
    given, surplus = [largest] + [least] * (amount - 1), total - largest - least * (amount - 1)
    while surplus > 0:
        free = [i for i in range(1, amount) if given[i] < largest] or [i for i in range(1, amount) if given[i] < limit]
        mass, budget = sum([loads[i] for i in free]), surplus
        for i in free:
            extra = min(limit - given[i], max(1, budget * loads[i] // mass), surplus)
            given[i] = given[i] + extra
            surplus = surplus - extra
    return np.array(given)


def normal_values(rng, shape, width, limit, cuts=(), held_as=jnp.bfloat16):
    entries = width * jax.random.normal(rng, shape, jnp.float32)
    if cuts:
        entries = entries * shard_levels(rng, shape, cuts, -0.22, 0.18)
    return jnp.clip(entries, -limit, limit).astype(held_as)


def setup_inputs(seed: int = 0) -> dict:
    keys = jax.random.split(jax.random.key(seed), 9)
    state = normal_values(keys[0], (4, NX, NY, NZ), 1.0, 6.0, ((1, 128),), jnp.float32)
    sample_cell = draw_sample_cell(jax.random.fold_in(keys[8], 71), 0)
    sample_frac = jnp.clip(1.0 * jax.random.uniform(keys[2], (3, EXCH), jnp.float32) ** shard_levels(keys[2], (3, EXCH), ((1, 128),), -0.2, 0.2), 0.0, 1.0)
    sample_owner_keys = jax.random.split(jax.random.fold_in(keys[3], 1), EXCH // EP_DEV)
    sample_owner_turns = jax.random.permutation(jax.random.fold_in(keys[3], 3), EXCH // EP_DEV)
    sample_owner = jax.vmap(lambda own, number: deal_out(jax.random.fold_in(keys[3], 2), own, number, EP_DEV, N_BLK, 1, CAP, 2))(sample_owner_keys, sample_owner_turns).reshape((EXCH, 1))
    face_angles = jnp.clip(jax.random.uniform(keys[4], (2, FACE_SLOTS), jnp.float32, -3.140625, 3.140625), -3.140625, 3.140625)
    face_height = jnp.clip(jnp.exp(math.log(0.5) - 2.3025851 * jax.random.uniform(keys[5], (FACE_SLOTS,), jnp.float32) ** shard_levels(keys[5], (FACE_SLOTS,), ((0, 128),), -0.2, 0.2)), 0.05, 0.5)
    wall_temp = normal_values(keys[6], (FACE_SLOTS,), 1.0, 6.0, ((0, 128),), jnp.float32)
    face_visc = jnp.clip(jnp.exp(math.log(0.05) - 2.3025851 * jax.random.uniform(keys[7], (FACE_SLOTS,), jnp.float32) ** shard_levels(keys[7], (FACE_SLOTS,), ((0, 128),), -0.2, 0.2)), 0.005, 0.05)
    return dict(state=state, sample_cell=sample_cell, sample_frac=sample_frac, sample_owner=sample_owner, face_angles=face_angles, face_height=face_height, wall_temp=wall_temp, face_visc=face_visc)


time_step = 0.1
grid_viscosity = 0.2
karman = 0.41
prandtl = 0.72
turb_prandtl = 0.9
speed_floor = 0.5

def transport(padded):
    center = padded[:, 1:-1]
    velocity = center[0:3]
    framed = jnp.pad(center, ((0, 0), (0, 0), (1, 1), (1, 1)))
    east_side = padded[:, 2:]
    west_side = padded[:, :-2]
    north_side = framed[:, :, 2:, 1:-1]
    south_side = framed[:, :, :-2, 1:-1]
    upper_side = framed[:, :, 1:-1, 2:]
    lower_side = framed[:, :, 1:-1, :-2]
    advect = velocity[0] * (east_side - west_side) + velocity[1] * (north_side - south_side) + velocity[2] * (upper_side - lower_side)
    spread = east_side + west_side + north_side + south_side + upper_side + lower_side - 6.0 * center
    return -0.5 * advect + grid_viscosity * spread

def wrapped(field):
    return jnp.concatenate([field[:, -1:], field, field[:, :1]], axis=1)

def corner_factor(fraction, upper_flag):
    if upper_flag:
        return fraction
    return 1.0 - fraction

def corners(base_cell, fraction, plane_cells, line_cells):
    corner_cells = []
    corner_weights = []
    for step_x in (0, 1):
        for step_y in (0, 1):
            for step_z in (0, 1):
                corner_cells.append(base_cell + step_x * plane_cells + step_y * line_cells + step_z)
                corner_weights.append(corner_factor(fraction[0], step_x) * corner_factor(fraction[1], step_y) * corner_factor(fraction[2], step_z))
    return (jnp.stack(corner_cells), jnp.stack(corner_weights))

def slot_index(owners, groups, capacity):
    onehot = (owners[:, None] == jnp.arange(groups, dtype=jnp.int32)[None, :]).astype(jnp.int32)
    before = jnp.cumsum(onehot, axis=0) - onehot
    position = lax.optimization_barrier(jnp.sum(before * onehot, axis=1))
    return owners * capacity + position

def wall_model(sample, angles, height, wall_temp, viscosity):
    normal = jnp.stack([jnp.sin(angles[0]) * jnp.cos(angles[1]), jnp.sin(angles[0]) * jnp.sin(angles[1]), jnp.cos(angles[0])])
    normal_speed = lax.optimization_barrier(jnp.sum(sample[0:3] * normal, axis=0))
    tangent = sample[0:3] - normal_speed[None] * normal
    tangent_speed = jnp.maximum(jnp.sqrt(lax.optimization_barrier(jnp.sum(tangent * tangent, axis=0))), speed_floor)
    direction = tangent / tangent_speed[None]
    ladder = (jnp.arange(NPTS, dtype=jnp.float32) + 0.5) / NPTS
    heights = height[None] * (ladder * ladder)[:, None]
    quad_weights = height[None] * (2.0 * ladder / NPTS)[:, None]
    friction = jnp.sqrt(viscosity * tangent_speed / height)
    for newton_step in range(NEWTON):
        eddy_visc = viscosity[None] + karman * heights * friction[None]
        inverse_sum = lax.optimization_barrier(jnp.sum(quad_weights / eddy_visc, axis=0))
        slope_sum = lax.optimization_barrier(jnp.sum(quad_weights * karman * heights / (eddy_visc * eddy_visc), axis=0))
        residual = friction * friction * inverse_sum - tangent_speed
        derivative = 2.0 * friction * inverse_sum - friction * friction * slope_sum
        friction = friction - residual / derivative
    conduct = viscosity[None] / prandtl + karman * heights * friction[None] / turb_prandtl
    resist = lax.optimization_barrier(jnp.sum(quad_weights / conduct, axis=0))
    heat_flux = (sample[3] - wall_temp) / resist
    stress = (friction * friction)[None] * direction
    return jnp.concatenate([stress, heat_flux[None]], axis=0)

def reference(state, sample_cell, sample_frac, sample_owner, face_angles, face_height, wall_temp, face_visc):
    middle = state + time_step * transport(wrapped(state))
    final_state = 0.5 * state + 0.5 * (middle + time_step * transport(wrapped(middle)))
    flat = middle.reshape(4, N_BLK, CX * NY * NZ)
    cells_dev = sample_cell.reshape(N_BLK, EP_DEV)
    frac_dev = sample_frac.reshape(3, N_BLK, EP_DEV)
    corner_cells, corner_weights = corners(cells_dev, frac_dev, NY * NZ, NZ)
    device_rows = jnp.arange(N_BLK, dtype=jnp.int32)[:, None]
    lookup = jnp.transpose(corner_cells, (1, 0, 2)).reshape(N_BLK, 8 * EP_DEV)
    values = flat[:, device_rows, lookup].reshape(4, N_BLK, 8, EP_DEV)
    sampled = lax.optimization_barrier(jnp.sum(values * jnp.transpose(corner_weights, (1, 0, 2))[None], axis=2)).reshape(4, EXCH)
    owners_dev = sample_owner[:, 0].reshape(N_BLK, EP_DEV)
    slots = jax.vmap(lambda owners: slot_index(owners, N_BLK, CAP))(owners_dev)
    position = slots - owners_dev * CAP
    column = (owners_dev * (N_BLK * CAP) + device_rows * CAP + position).reshape(EXCH).astype(jnp.int32)
    wall_flux = wall_model(sampled, face_angles[:, column], face_height[column], wall_temp[column], face_visc[column])
    return (final_state, wall_flux)
```

```python
import functools
import jax
import jax.numpy as jnp
from jax import lax
from jax.experimental import pallas as pl
from jax.experimental.pallas import tpu as pltpu
from jax.sharding import PartitionSpec as P

CX = 16
NY = 128
NZ = 256
POINTS = 512
NPTS = 64
NEWTON = 3
CAP = 8
COMPS = 4
LANES = 128
HALVES = NZ // LANES
PITCH = NY + 8
BLOCKS = HALVES * COMPS
LAYER = BLOCKS * PITCH
TILES = NY // 8
SHEET = BLOCKS * NY

time_step = 0.1
grid_viscosity = 0.2
karman = 0.41
prandtl = 0.72
turb_prandtl = 0.9
speed_floor = 0.5


def load8(flat, base, pitch):
    return [[flat[pl.ds(base + (h * COMPS + c) * pitch, 8), :] for c in range(COMPS)] for h in range(HALVES)]


def load8a(flat, base, pitch):
    return [
        [flat[pl.ds(pl.multiple_of(base + (h * COMPS + c) * pitch, 8), 8), :] for c in range(COMPS)]
        for h in range(HALVES)
    ]


def store8(flat, base, pitch, tiles):
    for h in range(HALVES):
        for c in range(COMPS):
            flat[pl.ds(pl.multiple_of(base + (h * COMPS + c) * pitch, 8), 8), :] = tiles[h][c]


def base_of(layer, yb):
    return layer * LAYER + yb * 8 + 8


def shifted(tiles):
    lane = lax.broadcasted_iota(jnp.int32, (8, LANES), 1)
    upper = [[None] * COMPS for _ in range(HALVES)]
    lower = [[None] * COMPS for _ in range(HALVES)]
    for c in range(COMPS):
        r0 = pltpu.roll(tiles[0][c], LANES - 1, 1)
        r1 = pltpu.roll(tiles[1][c], LANES - 1, 1)
        l0 = pltpu.roll(tiles[0][c], 1, 1)
        l1 = pltpu.roll(tiles[1][c], 1, 1)
        upper[0][c] = jnp.where(lane == LANES - 1, r1, r0)
        upper[1][c] = r1
        lower[0][c] = l0
        lower[1][c] = jnp.where(lane == 0, l0, l1)
    return upper, lower


def coefficients(center, scale):
    lane = lax.broadcasted_iota(jnp.int32, (8, LANES), 1)
    rest = grid_viscosity * scale
    coefs = []
    for h in range(HALVES):
        minus, plus = [], []
        for d in range(3):
            drift = center[h][d] * (0.5 * scale)
            minus.append(rest - drift)
            plus.append(rest + drift)
        coefs.append((minus, plus))
    coefs[1][0][2] = jnp.where(lane == LANES - 1, 0.0, coefs[1][0][2])
    coefs[0][1][2] = jnp.where(lane == 0, 0.0, coefs[0][1][2])
    return coefs


def blend(sides, h, c, coefs):
    minus, plus = coefs[h]
    (east, west), (north, south), (upper, lower) = sides
    xs = minus[0] * east[h][c] + plus[0] * west[h][c]
    ys = minus[1] * north[h][c] + plus[1] * south[h][c]
    zs = minus[2] * upper[h][c] + plus[2] * lower[h][c]
    return (xs + ys) + zs


def middle_tile(s, su, sl, x, yb, shift_base, shift_pitch):
    b = base_of(x, yb)
    center = load8a(s, b, PITCH)
    sides = (
        (load8a(s, b + LAYER, PITCH), load8a(s, b - LAYER, PITCH)),
        (load8(s, b + 1, PITCH), load8(s, b - 1, PITCH)),
        (load8a(su, shift_base, shift_pitch), load8a(sl, shift_base, shift_pitch)),
    )
    coefs = coefficients(center, time_step)
    keep = 1.0 - 6.0 * grid_viscosity * time_step
    return [[blend(sides, h, c, coefs) + keep * center[h][c] for c in range(COMPS)] for h in range(HALVES)]


def final_tile(s, s_layer, m, mu, ml, x, yb, shift_base, east=None):
    b = base_of(x, yb)
    center = load8a(m, b, PITCH)
    if east is None:
        east = load8a(m, b + LAYER, PITCH)
    sides = (
        (east, load8a(m, b - LAYER, PITCH)),
        (load8(m, b + 1, PITCH), load8(m, b - 1, PITCH)),
        (load8a(mu, shift_base, NY), load8a(ml, shift_base, NY)),
    )
    coefs = coefficients(center, 0.5 * time_step)
    keep = 0.5 - 3.0 * grid_viscosity * time_step
    old = load8a(s, base_of(s_layer, yb), PITCH)
    return [
        [blend(sides, h, c, coefs) + (keep * center[h][c] + 0.5 * old[h][c]) for c in range(COMPS)]
        for h in range(HALVES)
    ]


def zero_pads(ref, layers):
    def body(x, carry):
        for h in range(HALVES):
            for c in range(COMPS):
                ref[x, h, c, 0:8, :] = jnp.zeros((8, LANES), jnp.float32)
        return carry

    lax.fori_loop(0, layers, body, 0)


def half_layer(array, x, h):
    return array.at[:, x, :, pl.ds(h * LANES, LANES)]


def interior(state, final, mid, S, M, F, SU, SL, MU, ML, in_sem, mid_sem, out_sem):
    def in_copy(x, h):
        return pltpu.make_async_copy(half_layer(state, x, h), S.at[x, h, :, pl.ds(8, NY), :], in_sem.at[x, h])

    def mid_copy(x):
        return pltpu.make_async_copy(M.at[x], mid.at[x], mid_sem.at[x])

    def out_copy(x, h):
        return pltpu.make_async_copy(F.at[x & 1, h], half_layer(final, x, h), out_sem.at[x & 1, h])

    for x in range(CX):
        for h in range(HALVES):
            in_copy(x, h).start()
    zero_pads(S, CX + 1)
    zero_pads(M, CX + 1)
    s = S.reshape((CX + 1) * LAYER, LANES)
    m = M.reshape((CX + 1) * LAYER, LANES)
    f = F.reshape(2 * SHEET, LANES)

    def landed(x):
        for h in range(HALVES):
            in_copy(x, h).wait()

    landed(0)
    landed(1)
    for yb in range(TILES):
        u, l = shifted(load8a(s, base_of(1, yb), PITCH))
        store8(SU, yb * 64, 8, u)
        store8(SL, yb * 64, 8, l)

    def sweep(x, with_final):
        mids = [middle_tile(s, SU, SL, x, yb, yb * 64, 8) for yb in range(TILES)]
        if with_final:
            rb = ((x - 1) & 1) * SHEET
            fins = [
                final_tile(s, x - 1, m, MU, ML, x - 1, yb, rb + yb * 8, mids[yb]) for yb in range(TILES)
            ]
        news = [shifted(load8a(s, base_of(x + 1, yb), PITCH)) for yb in range(TILES)]
        for yb in range(TILES):
            store8(m, base_of(x, yb), PITCH, mids[yb])
            if with_final:
                store8(f, ((x - 1) & 1) * SHEET + yb * 8, NY, fins[yb])
            store8(SU, yb * 64, 8, news[yb][0])
            store8(SL, yb * 64, 8, news[yb][1])
            u, l = shifted(mids[yb])
            store8(MU, (x & 1) * SHEET + yb * 8, NY, u)
            store8(ML, (x & 1) * SHEET + yb * 8, NY, l)

    def head(x, carry):
        landed(x + 1)
        sweep(x, False)
        mid_copy(x).start()
        return carry

    lax.fori_loop(1, 3, head, 0)

    def main(x, carry):
        landed(x + 1)

        @pl.when(x >= 5)
        def _():
            for h in range(HALVES):
                out_copy(x - 3, h).wait()

        sweep(x, True)
        mid_copy(x).start()
        for h in range(HALVES):
            out_copy(x - 1, h).start()
        return carry

    lax.fori_loop(3, CX - 1, main, 0)

    def drain(x, carry):
        mid_copy(x).wait()
        return carry

    lax.fori_loop(1, CX - 1, drain, 0)
    for x in (CX - 4, CX - 3):
        for h in range(HALVES):
            out_copy(x, h).wait()


def run_interior(state):
    f32 = jnp.float32
    field = (CX + 1, HALVES, COMPS, PITCH, LANES)
    return pl.pallas_call(
        interior,
        out_shape=(
            jax.ShapeDtypeStruct((COMPS, CX, NY, NZ), f32),
            jax.ShapeDtypeStruct((CX, HALVES, COMPS, PITCH, LANES), f32),
        ),
        in_specs=[pl.BlockSpec(memory_space=pl.ANY)],
        out_specs=(pl.BlockSpec(memory_space=pl.ANY), pl.BlockSpec(memory_space=pl.ANY)),
        scratch_shapes=[
            pltpu.VMEM(field, f32),
            pltpu.VMEM(field, f32),
            pltpu.VMEM((2, HALVES, COMPS, NY, LANES), f32),
            pltpu.VMEM((SHEET, LANES), f32),
            pltpu.VMEM((SHEET, LANES), f32),
            pltpu.VMEM((2 * SHEET, LANES), f32),
            pltpu.VMEM((2 * SHEET, LANES), f32),
            pltpu.SemaphoreType.DMA((CX, 2)),
            pltpu.SemaphoreType.DMA((CX,)),
            pltpu.SemaphoreType.DMA((2, 2)),
        ],
        compiler_params=pltpu.CompilerParams(vmem_limit_bytes=56 << 20),
        name="interior",
    )(state)


def face_values(owner_row, received):
    owners = lax.broadcasted_iota(jnp.int32, (LANES, POINTS), 0)
    hit = owners == owner_row
    before = lax.broadcasted_iota(jnp.int32, (POINTS, POINTS), 0) < lax.broadcasted_iota(
        jnp.int32, (POINTS, POINTS), 1
    )
    earlier = jnp.dot(
        hit.astype(jnp.bfloat16), before.astype(jnp.bfloat16), preferred_element_type=jnp.float32
    )
    rank = jnp.sum(jnp.where(hit, earlier, 0.0), axis=0, keepdims=True)
    picked = jnp.dot(
        jnp.transpose(received),
        hit.astype(jnp.float32),
        precision=lax.Precision.HIGHEST,
        preferred_element_type=jnp.float32,
    )
    slot = lax.broadcasted_iota(jnp.int32, (CAP, POINTS), 0).astype(jnp.float32) == rank
    return [
        jnp.sum(jnp.where(slot, picked[CAP * v : CAP * v + CAP], 0.0), axis=0, keepdims=True) for v in range(5)
    ]


def wall_model(sample, theta, phi, height, wall_temp, viscosity):
    sin_theta = jnp.sin(theta)
    normal = [sin_theta * jnp.cos(phi), sin_theta * jnp.sin(phi), jnp.cos(theta)]
    normal_speed = sample[0] * normal[0] + sample[1] * normal[1] + sample[2] * normal[2]
    tangent = [sample[d] - normal_speed * normal[d] for d in range(3)]
    length = jnp.sqrt(tangent[0] * tangent[0] + tangent[1] * tangent[1] + tangent[2] * tangent[2])
    tangent_speed = jnp.maximum(length, speed_floor)
    ladder = (lax.broadcasted_iota(jnp.int32, (NPTS, POINTS), 0).astype(jnp.float32) + 0.5) / NPTS
    heights = height * (ladder * ladder)
    quad_weights = height * (ladder * (2.0 / NPTS))
    rise = karman * heights
    slope_weights = quad_weights * rise
    friction = jnp.sqrt(viscosity * tangent_speed / height)
    for newton_step in range(NEWTON):
        inverse = 1.0 / (viscosity + rise * friction)
        inverse_sum = jnp.sum(quad_weights * inverse, axis=0, keepdims=True)
        slope_sum = jnp.sum(slope_weights * (inverse * inverse), axis=0, keepdims=True)
        residual = friction * friction * inverse_sum - tangent_speed
        derivative = 2.0 * friction * inverse_sum - friction * friction * slope_sum
        friction = friction - residual / derivative
    conduct = viscosity / prandtl + rise * (friction / turb_prandtl)
    resist = jnp.sum(quad_weights / conduct, axis=0, keepdims=True)
    stress = friction * friction / tangent_speed
    return [stress * tangent[0], stress * tangent[1], stress * tangent[2], (sample[3] - wall_temp) / resist]


UNROLL = 32


def edges(
    cells, fracs, owner, received, state, mid, west_halo, east_halo, begun, final, flux,
    S, M, F, SU, SL, MU, ML, Q, in_sem, mid_sem, out_sem,
):
    sources = (
        (west_halo, 0), (west_halo, 1), (state, 0), (state, 1),
        (state, CX - 2), (state, CX - 1), (east_halo, 0), (east_halo, 1),
    )

    def in_copy(k, h):
        array, x = sources[k]
        return pltpu.make_async_copy(half_layer(array, x, h), S.at[k, h, :, pl.ds(8, NY), :], in_sem.at[k, h])

    def mid_copy(x):
        return pltpu.make_async_copy(mid.at[x], M.at[x + 1], mid_sem.at[x])

    for k in range(8):
        for h in range(HALVES):
            in_copy(k, h).start()
    for x in (1, 2, 13, 14):
        mid_copy(x).start()
    for x in range(3, 13):
        mid_copy(x).start()
    zero_pads(S, 9)
    for x in (0, 1, CX, CX + 1, CX + 2):
        for h in range(HALVES):
            for c in range(COMPS):
                M[x, h, c, 0:8, :] = jnp.zeros((8, LANES), jnp.float32)
    s = S.reshape(9 * LAYER, LANES)
    m = M.reshape((CX + 3) * LAYER, LANES)
    f = F.reshape(4 * SHEET, LANES)
    values = face_values(owner[...], received[...])
    for k in range(8):
        for h in range(HALVES):
            in_copy(k, h).wait()

    def s_layer(n):
        return 1 + (n & 1) + (n >> 1) * 4

    def m_layer(n):
        return (n & 1) + (n >> 1) * CX

    def roll_state(n, carry):
        for yb in range(TILES):
            u, l = shifted(load8a(s, base_of(s_layer(n), yb), PITCH))
            store8(SU, n * SHEET + yb * 8, NY, u)
            store8(SL, n * SHEET + yb * 8, NY, l)
        return carry

    lax.fori_loop(0, 4, roll_state, 0)

    def middle(n, carry):
        for yb in range(TILES):
            tile = middle_tile(s, SU, SL, s_layer(n), yb, n * SHEET + yb * 8, NY)
            store8(m, base_of(m_layer(n), yb), PITCH, tile)
        return carry

    lax.fori_loop(0, 4, middle, 0)
    for x in (1, 2, 13, 14):
        mid_copy(x).wait()

    def final_layer(n):
        return (n & 1) + (n >> 1) * (CX - 2)

    def roll_mid(n, carry):
        for yb in range(TILES):
            u, l = shifted(load8a(m, base_of(final_layer(n) + 1, yb), PITCH))
            store8(MU, n * SHEET + yb * 8, NY, u)
            store8(ML, n * SHEET + yb * 8, NY, l)
        return carry

    lax.fori_loop(0, 4, roll_mid, 0)

    def out_copy(n, h):
        return pltpu.make_async_copy(F.at[n, h], half_layer(final, final_layer(n), h), out_sem.at[n, h])

    def last(n, carry):
        for yb in range(TILES):
            tile = final_tile(s, 2 + n, m, MU, ML, final_layer(n) + 1, yb, n * SHEET + yb * 8)
            store8(f, n * SHEET + yb * 8, NY, tile)
        for h in range(HALVES):
            out_copy(n, h).start()
        return carry

    lax.fori_loop(0, 4, last, 0)
    for x in range(3, 13):
        mid_copy(x).wait()

    lane = lax.broadcasted_iota(jnp.int32, (8, LANES), 1)
    along = lane + LANES * (lax.broadcasted_iota(jnp.int32, (8, LANES), 0) // COMPS)

    def points(group, acc):
        total = acc
        first = group * UNROLL
        for p in range(UNROLL):
            e = first + p
            cell = cells[e]
            row = (lax.shift_right_logical(cell, 15) + 1) * LAYER + 8 + (lax.shift_right_logical(cell, 8) & (NY - 1))
            k = cell & (NZ - 1)
            fx, fy, fz = fracs[0, e], fracs[1, e], fracs[2, e]
            near0 = m[pl.ds(row, 8, stride=PITCH), :]
            near1 = m[pl.ds(row + 1, 8, stride=PITCH), :]
            far0 = m[pl.ds(row + LAYER, 8, stride=PITCH), :]
            far1 = m[pl.ds(row + LAYER + 1, 8, stride=PITCH), :]
            wide = (1.0 - fx) * ((1.0 - fy) * near0 + fy * near1) + fx * ((1.0 - fy) * far0 + fy * far1)
            depth = jnp.where(along == k, 1.0 - fz, jnp.where(along == k + 1, fz, 0.0))
            value = jnp.sum(wide * depth, axis=1, keepdims=True)
            total = jnp.where(lane == (e & (LANES - 1)), value, total)
        return total

    zero = jnp.zeros((8, LANES), jnp.float32)
    for q in range(POINTS // LANES):
        per = LANES // UNROLL
        got = lax.fori_loop(q * per, q * per + per, points, zero)
        Q[:, q * LANES : (q + 1) * LANES] = got
    both = Q[...]
    sampled = both[0:COMPS] + both[COMPS : 2 * COMPS]
    sample = [sampled[c : c + 1] for c in range(COMPS)]
    rows = wall_model(sample, *values)
    for c in range(COMPS):
        flux[c : c + 1, :] = rows[c]
    for n in range(4):
        for h in range(HALVES):
            out_copy(n, h).wait()


def run_edges(cells, fracs, owner, received, state, mid, west_halo, east_halo, begun):
    f32 = jnp.float32
    smem = pl.BlockSpec(memory_space=pltpu.SMEM)
    vmem = pl.BlockSpec(memory_space=pltpu.VMEM)
    hbm = pl.BlockSpec(memory_space=pl.ANY)
    return pl.pallas_call(
        edges,
        out_shape=(
            jax.ShapeDtypeStruct((COMPS, CX, NY, NZ), f32),
            jax.ShapeDtypeStruct((COMPS, POINTS), f32),
        ),
        in_specs=[smem, smem, vmem, vmem, hbm, hbm, hbm, hbm, hbm],
        out_specs=(hbm, vmem),
        input_output_aliases={8: 0},
        scratch_shapes=[
            pltpu.VMEM((9, HALVES, COMPS, PITCH, LANES), f32),
            pltpu.VMEM((CX + 3, HALVES, COMPS, PITCH, LANES), f32),
            pltpu.VMEM((4, HALVES, COMPS, NY, LANES), f32),
            pltpu.VMEM((4 * SHEET, LANES), f32),
            pltpu.VMEM((4 * SHEET, LANES), f32),
            pltpu.VMEM((4 * SHEET, LANES), f32),
            pltpu.VMEM((4 * SHEET, LANES), f32),
            pltpu.VMEM((8, POINTS), f32),
            pltpu.SemaphoreType.DMA((8, 2)),
            pltpu.SemaphoreType.DMA((CX,)),
            pltpu.SemaphoreType.DMA((4, 2)),
        ],
        compiler_params=pltpu.CompilerParams(vmem_limit_bytes=56 << 20),
        name="edges",
    )(cells, fracs, owner, received, state, mid, west_halo, east_halo, begun)


def on_device(
    state, sample_cell, sample_frac, sample_owner, face_angles, face_height, wall_temp, face_visc
):
    count = lax.axis_size("blk")
    ahead = [(i, (i + 1) % count) for i in range(count)]
    back = [((i + 1) % count, i) for i in range(count)]
    west_halo = lax.ppermute(state[:, CX - 2 :], "blk", ahead)
    east_halo = lax.ppermute(state[:, :2], "blk", back)
    faces = jnp.concatenate([face_angles, face_height[None], wall_temp[None], face_visc[None]], axis=0)
    faces = faces.reshape(5, count, CAP).transpose(1, 0, 2).reshape(count, 5 * CAP)
    faces = jnp.pad(faces, ((0, 0), (0, LANES - 5 * CAP)))
    received = lax.all_to_all(faces, "blk", split_axis=0, concat_axis=0, tiled=True)
    begun, mid = run_interior(state)
    owner = sample_owner.reshape(1, POINTS)
    return run_edges(sample_cell, sample_frac, owner, received, state, mid, west_halo, east_halo, begun)


def solution(mesh):
    placed = (
        P(None, "blk", None, None),
        P("blk"),
        P(None, "blk"),
        P("blk", None),
        P(None, "blk"),
        P("blk"),
        P("blk"),
        P("blk"),
    )
    return jax.shard_map(
        on_device,
        mesh=mesh,
        in_specs=placed,
        out_specs=(P(None, "blk", None, None), P(None, "blk")),
        check_vma=False,
    )
```

```python
import functools
import jax
import jax.numpy as jnp
from jax import lax
from jax.experimental import pallas as pl
from jax.experimental.pallas import tpu as pltpu
from jax.sharding import PartitionSpec as P

CX = 16
NY = 128
NZ = 256
POINTS = 512
NPTS = 64
NEWTON = 3
CAP = 8
COMPS = 4
LANES = 128
HALVES = NZ // LANES
PITCH = NY + 8
BLOCKS = HALVES * COMPS
LAYER = BLOCKS * PITCH
TILES = NY // 8
SHEET = BLOCKS * NY

time_step = 0.1
grid_viscosity = 0.2
karman = 0.41
prandtl = 0.72
turb_prandtl = 0.9
speed_floor = 0.5


def load8(flat, base, pitch):
    return [[flat[pl.ds(base + (h * COMPS + c) * pitch, 8), :] for c in range(COMPS)] for h in range(HALVES)]


def load8a(flat, base, pitch):
    return [
        [flat[pl.ds(pl.multiple_of(base + (h * COMPS + c) * pitch, 8), 8), :] for c in range(COMPS)]
        for h in range(HALVES)
    ]


def store8(flat, base, pitch, tiles):
    for h in range(HALVES):
        for c in range(COMPS):
            flat[pl.ds(pl.multiple_of(base + (h * COMPS + c) * pitch, 8), 8), :] = tiles[h][c]


def base_of(layer, yb):
    return layer * LAYER + yb * 8 + 8


def shifted(tiles):
    lane = lax.broadcasted_iota(jnp.int32, (8, LANES), 1)
    upper = [[None] * COMPS for _ in range(HALVES)]
    lower = [[None] * COMPS for _ in range(HALVES)]
    for c in range(COMPS):
        r0 = pltpu.roll(tiles[0][c], LANES - 1, 1)
        r1 = pltpu.roll(tiles[1][c], LANES - 1, 1)
        l0 = pltpu.roll(tiles[0][c], 1, 1)
        l1 = pltpu.roll(tiles[1][c], 1, 1)
        upper[0][c] = jnp.where(lane == LANES - 1, r1, r0)
        upper[1][c] = r1
        lower[0][c] = l0
        lower[1][c] = jnp.where(lane == 0, l0, l1)
    return upper, lower


def coefficients(center, scale):
    lane = lax.broadcasted_iota(jnp.int32, (8, LANES), 1)
    rest = grid_viscosity * scale
    coefs = []
    for h in range(HALVES):
        minus, plus = [], []
        for d in range(3):
            drift = center[h][d] * (0.5 * scale)
            minus.append(rest - drift)
            plus.append(rest + drift)
        coefs.append((minus, plus))
    coefs[1][0][2] = jnp.where(lane == LANES - 1, 0.0, coefs[1][0][2])
    coefs[0][1][2] = jnp.where(lane == 0, 0.0, coefs[0][1][2])
    return coefs


def blend(sides, h, c, coefs):
    minus, plus = coefs[h]
    (east, west), (north, south), (upper, lower) = sides
    xs = minus[0] * east[h][c] + plus[0] * west[h][c]
    ys = minus[1] * north[h][c] + plus[1] * south[h][c]
    zs = minus[2] * upper[h][c] + plus[2] * lower[h][c]
    return (xs + ys) + zs


def middle_tile(s, m, su, sl, x, yb):
    b = base_of(x + 2, yb)
    center = load8a(s, b, PITCH)
    sides = (
        (load8a(s, b + LAYER, PITCH), load8a(s, b - LAYER, PITCH)),
        (load8(s, b + 1, PITCH), load8(s, b - 1, PITCH)),
        (load8a(su, yb * 8, NY), load8a(sl, yb * 8, NY)),
    )
    coefs = coefficients(center, time_step)
    keep = 1.0 - 6.0 * grid_viscosity * time_step
    tiles = [[blend(sides, h, c, coefs) + keep * center[h][c] for c in range(COMPS)] for h in range(HALVES)]
    store8(m, base_of(x + 1, yb), PITCH, tiles)


def final_tile(s, m, f, f_base, mu, ml, x, yb):
    b = base_of(x + 1, yb)
    center = load8a(m, b, PITCH)
    sides = (
        (load8a(m, b + LAYER, PITCH), load8a(m, b - LAYER, PITCH)),
        (load8(m, b + 1, PITCH), load8(m, b - 1, PITCH)),
        (load8a(mu, yb * 8, NY), load8a(ml, yb * 8, NY)),
    )
    coefs = coefficients(center, 0.5 * time_step)
    keep = 0.5 - 3.0 * grid_viscosity * time_step
    old = load8a(s, base_of(x + 2, yb), PITCH)
    tiles = [
        [blend(sides, h, c, coefs) + (keep * center[h][c] + 0.5 * old[h][c]) for c in range(COMPS)]
        for h in range(HALVES)
    ]
    store8(f, f_base + yb * 8, NY, tiles)


def roll_tile(field, layer, yb, u_ref, l_ref):
    u, l = shifted(load8a(field, base_of(layer, yb), PITCH))
    store8(u_ref, yb * 8, NY, u)
    store8(l_ref, yb * 8, NY, l)


def zero_pads(ref, layers):
    def body(x, carry):
        for h in range(HALVES):
            for c in range(COMPS):
                ref[x, h, c, 0:8, :] = jnp.zeros((8, LANES), jnp.float32)
        return carry

    lax.fori_loop(0, layers, body, 0)


def half_layer(array, x, h):
    return array.at[:, x, :, pl.ds(h * LANES, LANES)]


S_SHAPE = (CX + 5, HALVES, COMPS, PITCH, LANES)
M_SHAPE = (CX + 3, HALVES, COMPS, PITCH, LANES)
RIM_SHAPE = (COMPS, 2, NY, NZ)
LAG = 3

hbm_spec = pl.BlockSpec(memory_space=pl.ANY)
vmem_spec = pl.BlockSpec(memory_space=pltpu.VMEM)
smem_spec = pl.BlockSpec(memory_space=pltpu.SMEM)
sheet = pltpu.VMEM((SHEET, LANES), jnp.float32)


def in_hbm(x):
    return pltpu.with_memory_space_constraint(x, pltpu.HBM)


def on_chip(x):
    return pltpu.with_memory_space_constraint(x, pltpu.VMEM)


def packed_faces(rows):
    lane = lax.broadcasted_iota(jnp.int32, (LANES, LANES), 1)
    sub = lax.broadcasted_iota(jnp.int32, (LANES, LANES), 0)
    per = LANES // CAP
    mine = lax.shift_right_logical(lane, 3) == (sub & (per - 1))
    left, right = [], []
    for v, row in enumerate(rows):
        spread = jnp.concatenate(
            [jnp.broadcast_to(row[:, q * LANES : (q + 1) * LANES], (per, LANES)) for q in range(CAP)], axis=0
        )
        left.append(jnp.where(mine, spread, 0.0))
        right.append(((sub & (CAP - 1)) + v * CAP == lane).astype(jnp.float32))
    return jnp.dot(
        jnp.concatenate(left, axis=1),
        jnp.concatenate(right, axis=0),
        precision=lax.Precision.HIGHEST,
        preferred_element_type=jnp.float32,
    )


def opening(state, angles, height, temp, visc, to_west, to_east, packed, rim_sem):
    def rim_copy(k, c):
        if k == 0:
            return pltpu.make_async_copy(state.at[c, pl.ds(0, 2)], to_west.at[c], rim_sem.at[0, c])
        return pltpu.make_async_copy(state.at[c, pl.ds(CX - 2, 2)], to_east.at[c], rim_sem.at[1, c])

    for k in range(2):
        for c in range(COMPS):
            rim_copy(k, c).start()
    packed[...] = packed_faces([angles[0:1, :], angles[1:2, :], height[...], temp[...], visc[...]])
    for k in range(2):
        for c in range(COMPS):
            rim_copy(k, c).wait()


def run_opening(state, angles, height, temp, visc):
    f32 = jnp.float32
    return pl.pallas_call(
        opening,
        out_shape=(
            pltpu.VMEM(RIM_SHAPE, f32),
            pltpu.VMEM(RIM_SHAPE, f32),
            jax.ShapeDtypeStruct((LANES, LANES), f32),
        ),
        in_specs=[hbm_spec, vmem_spec, vmem_spec, vmem_spec, vmem_spec],
        out_specs=(vmem_spec, vmem_spec, vmem_spec),
        scratch_shapes=[pltpu.SemaphoreType.DMA((2, COMPS))],
        name="opening",
    )(in_hbm(state), angles, height, temp, visc)


def interior(
    state, S, M, final, F, SU0, SL0, SU1, SL1, MU0, ML0, MU1, ML1, in_sem, out_sem
):
    def in_copy(x, h):
        return pltpu.make_async_copy(half_layer(state, x, h), S.at[x + 2, h, :, pl.ds(8, NY), :], in_sem.at[x, h])

    def out_copy(y, h):
        return pltpu.make_async_copy(F.at[y - 2, h], half_layer(final, y, h), out_sem.at[y - 2, h])

    for x in range(CX):
        for h in range(HALVES):
            in_copy(x, h).start()
    zero_pads(S, CX + 5)
    zero_pads(M, CX + 3)
    s = S.reshape((CX + 5) * LAYER, LANES)
    m = M.reshape((CX + 3) * LAYER, LANES)
    f = F.reshape((CX - 4) * SHEET, LANES)
    state_rolled = ((SU0, SL0), (SU1, SL1))
    mid_rolled = ((MU0, ML0), (MU1, ML1))

    def landed(x):
        for h in range(HALVES):
            in_copy(x, h).wait()

    landed(0)
    landed(1)
    for yb in range(TILES):
        roll_tile(s, 3, yb, *state_rolled[1])

    def step(x, y, odd_x, odd_y, next_mid=None):
        for yb in range(TILES):
            if y is not None:
                final_tile(s, m, f, (y - 2) * SHEET, *mid_rolled[odd_y], y, yb)
            if next_mid is not None:
                roll_tile(m, next_mid + 1, yb, *mid_rolled[0 if y is None else 1 - odd_y])
        for yb in range(TILES):
            if x is not None:
                middle_tile(s, m, *state_rolled[odd_x], x, yb)
                roll_tile(s, x + 3, yb, *state_rolled[1 - odd_x])
        if y is not None:
            for h in range(HALVES):
                out_copy(y, h).start()

    landed(2)
    step(1, None, 1, 0)
    landed(3)
    step(2, None, 0, 0)
    landed(4)
    step(3, None, 1, 0)
    landed(5)
    step(4, None, 0, 0, next_mid=2)

    def both(p, carry):
        x = 5 + 2 * p
        y = x - LAG
        landed(x + 1)
        step(x, y, 1, 0, next_mid=y + 1)
        landed(x + 2)
        step(x + 1, y + 1, 0, 1, next_mid=y + 2)
        return carry

    lax.fori_loop(0, (CX - 6) // 2, both, 0)
    step(None, CX - 4, 0, 0, next_mid=CX - 3)
    step(None, CX - 3, 0, 1)
    for y in range(2, CX - 2):
        for h in range(HALVES):
            out_copy(y, h).wait()


def run_interior(state):
    f32 = jnp.float32
    return pl.pallas_call(
        interior,
        out_shape=(
            pltpu.VMEM(S_SHAPE, f32),
            pltpu.VMEM(M_SHAPE, f32),
            jax.ShapeDtypeStruct((COMPS, CX, NY, NZ), f32),
        ),
        in_specs=[hbm_spec],
        out_specs=(vmem_spec, vmem_spec, hbm_spec),
        scratch_shapes=[pltpu.VMEM((CX - 4, HALVES, COMPS, NY, LANES), f32)]
        + [sheet] * 8
        + [pltpu.SemaphoreType.DMA((CX, 2)), pltpu.SemaphoreType.DMA((CX - 4, 2))],
        compiler_params=pltpu.CompilerParams(vmem_limit_bytes=14 << 20),
        name="interior",
    )(in_hbm(state))


def edges(
    cells, fracs, S_in, M_in, west_halo, east_halo, begun, S, M, final, sampled,
    F, SU0, SL0, SU1, SL1, MU, ML, in_sem, out_sem,
):
    def in_copy(k, h):
        array = west_halo if k < 2 else east_halo
        layer = k if k < 2 else CX + k
        return pltpu.make_async_copy(
            half_layer(array, k & 1, h), S.at[layer, h, :, pl.ds(8, NY), :], in_sem.at[k, h]
        )

    for k in range(4):
        for h in range(HALVES):
            in_copy(k, h).start()
    s = S.reshape((CX + 5) * LAYER, LANES)
    m = M.reshape((CX + 3) * LAYER, LANES)
    f = F.reshape(4 * SHEET, LANES)
    rolled = ((SU0, SL0), (SU1, SL1))

    def mid_refs(n):
        return MU.at[pl.ds(n * SHEET, SHEET)], ML.at[pl.ds(n * SHEET, SHEET)]

    for yb in range(TILES):
        roll_tile(s, 2, yb, *rolled[0])
        roll_tile(m, 2, yb, *mid_refs(1))
    for k in range(4):
        for h in range(HALVES):
            in_copy(k, h).wait()
    for yb in range(TILES):
        middle_tile(s, m, *rolled[0], 0, yb)
        roll_tile(s, CX + 1, yb, *rolled[1])
        roll_tile(m, CX - 1, yb, *mid_refs(2))
    for yb in range(TILES):
        middle_tile(s, m, *rolled[1], CX - 1, yb)
        roll_tile(s, 1, yb, *rolled[0])
        roll_tile(m, 1, yb, *mid_refs(0))
    for yb in range(TILES):
        middle_tile(s, m, *rolled[0], -1, yb)
        roll_tile(s, CX + 2, yb, *rolled[1])
        roll_tile(m, CX, yb, *mid_refs(3))
    for yb in range(TILES):
        middle_tile(s, m, *rolled[1], CX, yb)

    def final_layer(n):
        return (n & 1) + (n >> 1) * (CX - 2)

    def out_copy(n, h):
        return pltpu.make_async_copy(F.at[n, h], half_layer(final, final_layer(n), h), out_sem.at[n, h])

    lane = lax.broadcasted_iota(jnp.int32, (8, LANES), 1)
    along = lane + LANES * (lax.broadcasted_iota(jnp.int32, (8, LANES), 0) // COMPS)

    def sampled_at(e):
        cell = cells[e]
        row = (lax.shift_right_logical(cell, 15) + 1) * LAYER + 8 + (lax.shift_right_logical(cell, 8) & (NY - 1))
        k = cell & (NZ - 1)
        fx, fy, fz = fracs[0, e], fracs[1, e], fracs[2, e]
        near0 = m[pl.ds(row, 8, stride=PITCH), :]
        near1 = m[pl.ds(row + 1, 8, stride=PITCH), :]
        far0 = m[pl.ds(row + LAYER, 8, stride=PITCH), :]
        far1 = m[pl.ds(row + LAYER + 1, 8, stride=PITCH), :]
        wide = (1.0 - fx) * ((1.0 - fy) * near0 + fy * near1) + fx * ((1.0 - fy) * far0 + fy * far1)
        depth = jnp.where(along == k, 1.0 - fz, jnp.where(along == k + 1, fz, 0.0))
        return jnp.sum(wide * depth, axis=1, keepdims=True)

    def last(n, carry):
        total = jnp.zeros((8, LANES), jnp.float32)
        per = LANES // TILES
        for yb in range(TILES):
            final_tile(s, m, f, n * SHEET, *mid_refs(n), final_layer(n), yb)
            for p in range(yb * per, yb * per + per):
                total = jnp.where(lane == p, sampled_at(n * LANES + p), total)
        sampled[n] = total
        for h in range(HALVES):
            out_copy(n, h).start()
        return carry

    lax.fori_loop(0, 4, last, 0)
    for n in range(4):
        for h in range(HALVES):
            out_copy(n, h).wait()


def run_edges(cells, fracs, S, M, west_halo, east_halo, begun):
    f32 = jnp.float32
    outs = pl.pallas_call(
        edges,
        out_shape=(
            pltpu.VMEM(S_SHAPE, f32),
            pltpu.VMEM(M_SHAPE, f32),
            jax.ShapeDtypeStruct((COMPS, CX, NY, NZ), f32),
            pltpu.VMEM((POINTS // LANES, 8, LANES), f32),
        ),
        in_specs=[smem_spec, smem_spec, vmem_spec, vmem_spec, vmem_spec, vmem_spec, hbm_spec],
        out_specs=(vmem_spec, vmem_spec, hbm_spec, vmem_spec),
        input_output_aliases={2: 0, 3: 1, 6: 2},
        scratch_shapes=[pltpu.VMEM((4, HALVES, COMPS, NY, LANES), f32)]
        + [sheet] * 4
        + [
            pltpu.VMEM((4 * SHEET, LANES), f32),
            pltpu.VMEM((4 * SHEET, LANES), f32),
            pltpu.SemaphoreType.DMA((4, 2)),
            pltpu.SemaphoreType.DMA((4, 2)),
        ],
        compiler_params=pltpu.CompilerParams(vmem_limit_bytes=14 << 20),
        name="edges",
    )(cells, fracs, on_chip(S), on_chip(M), on_chip(west_halo), on_chip(east_halo), begun)
    return outs[2], outs[3]


def face_values(owner_row, received):
    owners = lax.broadcasted_iota(jnp.int32, (LANES, POINTS), 0)
    hit = owners == owner_row
    before = lax.broadcasted_iota(jnp.int32, (POINTS, POINTS), 0) < lax.broadcasted_iota(
        jnp.int32, (POINTS, POINTS), 1
    )
    earlier = jnp.dot(
        hit.astype(jnp.bfloat16), before.astype(jnp.bfloat16), preferred_element_type=jnp.float32
    )
    rank = jnp.sum(jnp.where(hit, earlier, 0.0), axis=0, keepdims=True)
    picked = jnp.dot(
        jnp.transpose(received),
        hit.astype(jnp.float32),
        precision=lax.Precision.HIGHEST,
        preferred_element_type=jnp.float32,
    )
    slot = lax.broadcasted_iota(jnp.int32, (CAP, POINTS), 0).astype(jnp.float32) == rank
    return [
        jnp.sum(jnp.where(slot, picked[CAP * v : CAP * v + CAP], 0.0), axis=0, keepdims=True) for v in range(5)
    ]


def wall_model(sample, theta, phi, height, wall_temp, viscosity):
    sin_theta = jnp.sin(theta)
    normal = [sin_theta * jnp.cos(phi), sin_theta * jnp.sin(phi), jnp.cos(theta)]
    normal_speed = sample[0] * normal[0] + sample[1] * normal[1] + sample[2] * normal[2]
    tangent = [sample[d] - normal_speed * normal[d] for d in range(3)]
    length = jnp.sqrt(tangent[0] * tangent[0] + tangent[1] * tangent[1] + tangent[2] * tangent[2])
    tangent_speed = jnp.maximum(length, speed_floor)
    ladder = (lax.broadcasted_iota(jnp.int32, (NPTS, POINTS), 0).astype(jnp.float32) + 0.5) / NPTS
    heights = height * (ladder * ladder)
    quad_weights = height * (ladder * (2.0 / NPTS))
    rise = karman * heights
    slope_weights = quad_weights * rise
    friction = jnp.sqrt(viscosity * tangent_speed / height)
    for newton_step in range(NEWTON):
        inverse = 1.0 / (viscosity + rise * friction)
        inverse_sum = jnp.sum(quad_weights * inverse, axis=0, keepdims=True)
        slope_sum = jnp.sum(slope_weights * (inverse * inverse), axis=0, keepdims=True)
        residual = friction * friction * inverse_sum - tangent_speed
        derivative = 2.0 * friction * inverse_sum - friction * friction * slope_sum
        friction = friction - residual / derivative
    conduct = viscosity / prandtl + rise * (friction / turb_prandtl)
    resist = jnp.sum(quad_weights / conduct, axis=0, keepdims=True)
    stress = friction * friction / tangent_speed
    return [stress * tangent[0], stress * tangent[1], stress * tangent[2], (sample[3] - wall_temp) / resist]


def walls(owner, received, sampled, flux):
    values = face_values(owner[...], received[...])
    both = jnp.concatenate([sampled[n] for n in range(POINTS // LANES)], axis=1)
    total = both[0:COMPS] + both[COMPS : 2 * COMPS]
    rows = wall_model([total[c : c + 1] for c in range(COMPS)], *values)
    for c in range(COMPS):
        flux[c : c + 1, :] = rows[c]


def run_walls(owner, received, sampled):
    return pl.pallas_call(
        walls,
        out_shape=jax.ShapeDtypeStruct((COMPS, POINTS), jnp.float32),
        in_specs=[vmem_spec] * 3,
        out_specs=vmem_spec,
        name="walls",
    )(owner, on_chip(received), on_chip(sampled))


def on_device(
    state, sample_cell, sample_frac, sample_owner, face_angles, face_height, wall_temp, face_visc
):
    count = lax.axis_size("blk")
    ahead = [(i, (i + 1) % count) for i in range(count)]
    back = [((i + 1) % count, i) for i in range(count)]
    to_west, to_east, packed = run_opening(
        state, face_angles, face_height.reshape(1, -1), wall_temp.reshape(1, -1), face_visc.reshape(1, -1)
    )
    west_halo = lax.ppermute(to_east, "blk", ahead)
    east_halo = lax.ppermute(to_west, "blk", back)
    received = lax.all_to_all(packed, "blk", split_axis=0, concat_axis=0, tiled=True)
    S, M, begun = run_interior(state)
    final, sampled = run_edges(sample_cell, sample_frac, S, M, west_halo, east_halo, begun)
    return final, run_walls(sample_owner.reshape(1, POINTS), received, sampled)


def solution(mesh):
    placed = (
        P(None, "blk", None, None),
        P("blk"),
        P(None, "blk"),
        P("blk", None),
        P(None, "blk"),
        P("blk"),
        P("blk"),
        P("blk"),
    )
    return jax.shard_map(
        on_device,
        mesh=mesh,
        in_specs=placed,
        out_specs=(P(None, "blk", None, None), P(None, "blk")),
        check_vma=False,
    )
```

```python
import functools
import jax
import jax.numpy as jnp
from jax import lax
from jax.experimental import pallas as pl
from jax.experimental.pallas import tpu as pltpu
from jax.sharding import PartitionSpec as P

CX = 16
NY = 128
NZ = 256
POINTS = 512
NPTS = 64
NEWTON = 3
CAP = 8
COMPS = 4
LANES = 128
HALVES = NZ // LANES
PITCH = NY + 8
BLOCKS = HALVES * COMPS
LAYER = BLOCKS * PITCH
TILES = NY // 8
SHEET = BLOCKS * NY

time_step = 0.1
grid_viscosity = 0.2
karman = 0.41
prandtl = 0.72
turb_prandtl = 0.9
speed_floor = 0.5


def load8(flat, base, pitch):
    return [[flat[pl.ds(base + (h * COMPS + c) * pitch, 8), :] for c in range(COMPS)] for h in range(HALVES)]


def load8a(flat, base, pitch):
    return [
        [flat[pl.ds(pl.multiple_of(base + (h * COMPS + c) * pitch, 8), 8), :] for c in range(COMPS)]
        for h in range(HALVES)
    ]


def store8(flat, base, pitch, tiles):
    for h in range(HALVES):
        for c in range(COMPS):
            flat[pl.ds(pl.multiple_of(base + (h * COMPS + c) * pitch, 8), 8), :] = tiles[h][c]


def base_of(layer, yb):
    return layer * LAYER + yb * 8 + 8


def shifted(tiles):
    lane = lax.broadcasted_iota(jnp.int32, (8, LANES), 1)
    upper = [[None] * COMPS for _ in range(HALVES)]
    lower = [[None] * COMPS for _ in range(HALVES)]
    for c in range(COMPS):
        r0 = pltpu.roll(tiles[0][c], LANES - 1, 1)
        r1 = pltpu.roll(tiles[1][c], LANES - 1, 1)
        l0 = pltpu.roll(tiles[0][c], 1, 1)
        l1 = pltpu.roll(tiles[1][c], 1, 1)
        upper[0][c] = jnp.where(lane == LANES - 1, r1, r0)
        upper[1][c] = r1
        lower[0][c] = l0
        lower[1][c] = jnp.where(lane == 0, l0, l1)
    return upper, lower


def coefficients(center, scale):
    lane = lax.broadcasted_iota(jnp.int32, (8, LANES), 1)
    rest = grid_viscosity * scale
    coefs = []
    for h in range(HALVES):
        minus, plus = [], []
        for d in range(3):
            drift = center[h][d] * (0.5 * scale)
            minus.append(rest - drift)
            plus.append(rest + drift)
        coefs.append((minus, plus))
    coefs[1][0][2] = jnp.where(lane == LANES - 1, 0.0, coefs[1][0][2])
    coefs[0][1][2] = jnp.where(lane == 0, 0.0, coefs[0][1][2])
    return coefs


def blend(sides, h, c, coefs):
    minus, plus = coefs[h]
    (east, west), (north, south), (upper, lower) = sides
    xs = minus[0] * east[h][c] + plus[0] * west[h][c]
    ys = minus[1] * north[h][c] + plus[1] * south[h][c]
    zs = minus[2] * upper[h][c] + plus[2] * lower[h][c]
    return (xs + ys) + zs


def middle_tile(s, su, sl, shift_base, x, yb):
    b = base_of(x + 2, yb)
    center = load8a(s, b, PITCH)
    sides = (
        (load8a(s, b + LAYER, PITCH), load8a(s, b - LAYER, PITCH)),
        (load8(s, b + 1, PITCH), load8(s, b - 1, PITCH)),
        (load8a(su, shift_base + yb * 8, NY), load8a(sl, shift_base + yb * 8, NY)),
    )
    coefs = coefficients(center, time_step)
    keep = 1.0 - 6.0 * grid_viscosity * time_step
    return [[blend(sides, h, c, coefs) + keep * center[h][c] for c in range(COMPS)] for h in range(HALVES)]


def final_tile(s, m, mu, ml, shift_base, x, yb, east=None):
    b = base_of(x + 1, yb)
    center = load8a(m, b, PITCH)
    sides = (
        (load8a(m, b + LAYER, PITCH) if east is None else east, load8a(m, b - LAYER, PITCH)),
        (load8(m, b + 1, PITCH), load8(m, b - 1, PITCH)),
        (load8a(mu, shift_base + yb * 8, NY), load8a(ml, shift_base + yb * 8, NY)),
    )
    coefs = coefficients(center, 0.5 * time_step)
    keep = 0.5 - 3.0 * grid_viscosity * time_step
    old = load8a(s, base_of(x + 2, yb), PITCH)
    return [
        [blend(sides, h, c, coefs) + (keep * center[h][c] + 0.5 * old[h][c]) for c in range(COMPS)]
        for h in range(HALVES)
    ]


def shifted_tile(field, layer, yb):
    return shifted(load8a(field, base_of(layer, yb), PITCH))


def store_shifted(u_ref, l_ref, base, pair):
    store8(u_ref, base, NY, pair[0])
    store8(l_ref, base, NY, pair[1])


def zero_pads(ref, layers):
    def body(x, carry):
        for h in range(HALVES):
            for c in range(COMPS):
                ref[x, h, c, 0:8, :] = jnp.zeros((8, LANES), jnp.float32)
        return carry

    lax.fori_loop(0, layers, body, 0)


def half_layer(array, x, h):
    return array.at[:, x, :, pl.ds(h * LANES, LANES)]


S_SHAPE = (CX + 5, HALVES, COMPS, PITCH, LANES)
M_SHAPE = (CX + 3, HALVES, COMPS, PITCH, LANES)
RIM_SHAPE = (COMPS, 2, NY, NZ)
LAG = 3

hbm_spec = pl.BlockSpec(memory_space=pl.ANY)
vmem_spec = pl.BlockSpec(memory_space=pltpu.VMEM)
smem_spec = pl.BlockSpec(memory_space=pltpu.SMEM)
sheet = pltpu.VMEM((SHEET, LANES), jnp.float32)


def in_hbm(x):
    return pltpu.with_memory_space_constraint(x, pltpu.HBM)


def on_chip(x):
    return pltpu.with_memory_space_constraint(x, pltpu.VMEM)


def packed_faces(rows):
    lane = lax.broadcasted_iota(jnp.int32, (LANES, LANES), 1)
    sub = lax.broadcasted_iota(jnp.int32, (LANES, LANES), 0)
    per = LANES // CAP
    mine = lax.shift_right_logical(lane, 3) == (sub & (per - 1))
    left, right = [], []
    for v, row in enumerate(rows):
        spread = jnp.concatenate(
            [jnp.broadcast_to(row[:, q * LANES : (q + 1) * LANES], (per, LANES)) for q in range(CAP)], axis=0
        )
        left.append(jnp.where(mine, spread, 0.0))
        right.append(((sub & (CAP - 1)) + v * CAP == lane).astype(jnp.float32))
    return jnp.dot(
        jnp.concatenate(left, axis=1),
        jnp.concatenate(right, axis=0),
        precision=lax.Precision.HIGHEST,
        preferred_element_type=jnp.float32,
    )


def opening(state, angles, height, temp, visc, to_west, to_east, packed, rim_sem):
    def rim_copy(k, c):
        if k == 0:
            return pltpu.make_async_copy(state.at[c, pl.ds(0, 2)], to_west.at[c], rim_sem.at[0, c])
        return pltpu.make_async_copy(state.at[c, pl.ds(CX - 2, 2)], to_east.at[c], rim_sem.at[1, c])

    for k in range(2):
        for c in range(COMPS):
            rim_copy(k, c).start()
    packed[...] = packed_faces([angles[0:1, :], angles[1:2, :], height[...], temp[...], visc[...]])
    for k in range(2):
        for c in range(COMPS):
            rim_copy(k, c).wait()


def run_opening(state, angles, height, temp, visc):
    f32 = jnp.float32
    return pl.pallas_call(
        opening,
        out_shape=(
            pltpu.VMEM(RIM_SHAPE, f32),
            pltpu.VMEM(RIM_SHAPE, f32),
            jax.ShapeDtypeStruct((LANES, LANES), f32),
        ),
        in_specs=[hbm_spec, vmem_spec, vmem_spec, vmem_spec, vmem_spec],
        out_specs=(vmem_spec, vmem_spec, vmem_spec),
        scratch_shapes=[pltpu.SemaphoreType.DMA((2, COMPS))],
        name="opening",
    )(in_hbm(state), angles, height, temp, visc)


def interior(state, S, M, final, F, SU, SL, MU, ML, in_sem, out_sem):
    def in_copy(x, h):
        return pltpu.make_async_copy(half_layer(state, x, h), S.at[x + 2, h, :, pl.ds(8, NY), :], in_sem.at[x, h])

    def out_copy(y, h):
        return pltpu.make_async_copy(F.at[y - 2, h], half_layer(final, y, h), out_sem.at[y - 2, h])

    for x in range(CX):
        for h in range(HALVES):
            in_copy(x, h).start()
    zero_pads(S, CX + 5)
    zero_pads(M, CX + 3)
    s = S.reshape((CX + 5) * LAYER, LANES)
    m = M.reshape((CX + 3) * LAYER, LANES)
    f = F.reshape((CX - 4) * SHEET, LANES)
    def landed(x):
        for h in range(HALVES):
            in_copy(x, h).wait()

    landed(0)
    landed(1)
    for yb in range(TILES):
        store_shifted(SU, SL, yb * 8, shifted_tile(s, 3, yb))

    def sweep(x, with_final):
        landed(x + 1)
        mids = [middle_tile(s, SU, SL, 0, x, yb) for yb in range(TILES)]
        if with_final:
            rb = ((x - 1) & 1) * SHEET
            fins = [final_tile(s, m, MU, ML, rb, x - 1, yb, mids[yb]) for yb in range(TILES)]
        news = [shifted_tile(s, x + 3, yb) for yb in range(TILES)]
        for yb in range(TILES):
            store8(m, base_of(x + 1, yb), PITCH, mids[yb])
            if with_final:
                store8(f, (x - 3) * SHEET + yb * 8, NY, fins[yb])
            store_shifted(SU, SL, yb * 8, news[yb])
            store_shifted(MU, ML, (x & 1) * SHEET + yb * 8, shifted(mids[yb]))
        if with_final:
            for h in range(HALVES):
                out_copy(x - 1, h).start()

    def head(x, carry):
        sweep(x, False)
        return carry

    def main(x, carry):
        sweep(x, True)
        return carry

    lax.fori_loop(1, 3, head, 0)
    lax.fori_loop(3, CX - 1, main, 0)
    for y in range(2, CX - 2):
        for h in range(HALVES):
            out_copy(y, h).wait()


def run_interior(state):
    f32 = jnp.float32
    return pl.pallas_call(
        interior,
        out_shape=(
            pltpu.VMEM(S_SHAPE, f32),
            pltpu.VMEM(M_SHAPE, f32),
            jax.ShapeDtypeStruct((COMPS, CX, NY, NZ), f32),
        ),
        in_specs=[hbm_spec],
        out_specs=(vmem_spec, vmem_spec, hbm_spec),
        scratch_shapes=[pltpu.VMEM((CX - 4, HALVES, COMPS, NY, LANES), f32), sheet, sheet]
        + [pltpu.VMEM((2 * SHEET, LANES), f32)] * 2
        + [pltpu.SemaphoreType.DMA((CX, 2)), pltpu.SemaphoreType.DMA((CX - 4, 2))],
        compiler_params=pltpu.CompilerParams(vmem_limit_bytes=14 << 20),
        name="interior",
    )(in_hbm(state))


def edges(
    cells, fracs, S_in, M_in, west_halo, east_halo, begun, S, M, final, sampled,
    F, SU0, SL0, SU1, SL1, MU, ML, in_sem, out_sem,
):
    def in_copy(k, h):
        array = west_halo if k < 2 else east_halo
        layer = k if k < 2 else CX + k
        return pltpu.make_async_copy(
            half_layer(array, k & 1, h), S.at[layer, h, :, pl.ds(8, NY), :], in_sem.at[k, h]
        )

    for k in range(4):
        for h in range(HALVES):
            in_copy(k, h).start()
    s = S.reshape((CX + 5) * LAYER, LANES)
    m = M.reshape((CX + 3) * LAYER, LANES)
    f = F.reshape(4 * SHEET, LANES)
    rolled = ((SU0, SL0), (SU1, SL1))

    def put_middle(su, sl, x, yb):
        store8(m, base_of(x + 1, yb), PITCH, middle_tile(s, su, sl, 0, x, yb))

    def put_shifted(field, layer, yb, u_ref, l_ref):
        store_shifted(u_ref, l_ref, yb * 8, shifted_tile(field, layer, yb))

    def mid_refs(n):
        return MU.at[pl.ds(n * SHEET, SHEET)], ML.at[pl.ds(n * SHEET, SHEET)]

    for yb in range(TILES):
        put_shifted(s, 2, yb, *rolled[0])
        put_shifted(m, 2, yb, *mid_refs(1))
    for k in range(4):
        for h in range(HALVES):
            in_copy(k, h).wait()
    for yb in range(TILES):
        put_middle(*rolled[0], 0, yb)
        put_shifted(s, CX + 1, yb, *rolled[1])
        put_shifted(m, CX - 1, yb, *mid_refs(2))
    for yb in range(TILES):
        put_middle(*rolled[1], CX - 1, yb)
        put_shifted(s, 1, yb, *rolled[0])
        put_shifted(m, 1, yb, *mid_refs(0))
    for yb in range(TILES):
        put_middle(*rolled[0], -1, yb)
        put_shifted(s, CX + 2, yb, *rolled[1])
        put_shifted(m, CX, yb, *mid_refs(3))
    for yb in range(TILES):
        put_middle(*rolled[1], CX, yb)

    def final_layer(n):
        return (n & 1) + (n >> 1) * (CX - 2)

    def out_copy(n, h):
        return pltpu.make_async_copy(F.at[n, h], half_layer(final, final_layer(n), h), out_sem.at[n, h])

    lane = lax.broadcasted_iota(jnp.int32, (8, LANES), 1)
    along = lane + LANES * (lax.broadcasted_iota(jnp.int32, (8, LANES), 0) // COMPS)

    def sampled_at(e):
        cell = cells[e]
        row = (lax.shift_right_logical(cell, 15) + 1) * LAYER + 8 + (lax.shift_right_logical(cell, 8) & (NY - 1))
        k = cell & (NZ - 1)
        fx, fy, fz = fracs[0, e], fracs[1, e], fracs[2, e]
        near0 = m[pl.ds(row, 8, stride=PITCH), :]
        near1 = m[pl.ds(row + 1, 8, stride=PITCH), :]
        far0 = m[pl.ds(row + LAYER, 8, stride=PITCH), :]
        far1 = m[pl.ds(row + LAYER + 1, 8, stride=PITCH), :]
        wide = (1.0 - fx) * ((1.0 - fy) * near0 + fy * near1) + fx * ((1.0 - fy) * far0 + fy * far1)
        depth = jnp.where(along == k, 1.0 - fz, jnp.where(along == k + 1, fz, 0.0))
        return jnp.sum(wide * depth, axis=1, keepdims=True)

    def last(n, carry):
        total = jnp.zeros((8, LANES), jnp.float32)
        per = LANES // TILES
        for yb in range(TILES):
            tile = final_tile(s, m, MU, ML, n * SHEET, final_layer(n), yb)
            store8(f, n * SHEET + yb * 8, NY, tile)
            for p in range(yb * per, yb * per + per):
                total = jnp.where(lane == p, sampled_at(n * LANES + p), total)
        sampled[n] = total
        for h in range(HALVES):
            out_copy(n, h).start()
        return carry

    lax.fori_loop(0, 4, last, 0)
    for n in range(4):
        for h in range(HALVES):
            out_copy(n, h).wait()


def run_edges(cells, fracs, S, M, west_halo, east_halo, begun):
    f32 = jnp.float32
    outs = pl.pallas_call(
        edges,
        out_shape=(
            pltpu.VMEM(S_SHAPE, f32),
            pltpu.VMEM(M_SHAPE, f32),
            jax.ShapeDtypeStruct((COMPS, CX, NY, NZ), f32),
            pltpu.VMEM((POINTS // LANES, 8, LANES), f32),
        ),
        in_specs=[smem_spec, smem_spec, vmem_spec, vmem_spec, vmem_spec, vmem_spec, hbm_spec],
        out_specs=(vmem_spec, vmem_spec, hbm_spec, vmem_spec),
        input_output_aliases={2: 0, 3: 1, 6: 2},
        scratch_shapes=[pltpu.VMEM((4, HALVES, COMPS, NY, LANES), f32)]
        + [sheet] * 4
        + [
            pltpu.VMEM((4 * SHEET, LANES), f32),
            pltpu.VMEM((4 * SHEET, LANES), f32),
            pltpu.SemaphoreType.DMA((4, 2)),
            pltpu.SemaphoreType.DMA((4, 2)),
        ],
        compiler_params=pltpu.CompilerParams(vmem_limit_bytes=14 << 20),
        name="edges",
    )(cells, fracs, on_chip(S), on_chip(M), on_chip(west_halo), on_chip(east_halo), begun)
    return outs[2], outs[3]


def face_values(owner_row, received):
    owners = lax.broadcasted_iota(jnp.int32, (LANES, POINTS), 0)
    hit = owners == owner_row
    before = lax.broadcasted_iota(jnp.int32, (POINTS, POINTS), 0) < lax.broadcasted_iota(
        jnp.int32, (POINTS, POINTS), 1
    )
    earlier = jnp.dot(
        hit.astype(jnp.bfloat16), before.astype(jnp.bfloat16), preferred_element_type=jnp.float32
    )
    rank = jnp.sum(jnp.where(hit, earlier, 0.0), axis=0, keepdims=True)
    picked = jnp.dot(
        jnp.transpose(received),
        hit.astype(jnp.float32),
        precision=lax.Precision.HIGHEST,
        preferred_element_type=jnp.float32,
    )
    slot = lax.broadcasted_iota(jnp.int32, (CAP, POINTS), 0).astype(jnp.float32) == rank
    return [
        jnp.sum(jnp.where(slot, picked[CAP * v : CAP * v + CAP], 0.0), axis=0, keepdims=True) for v in range(5)
    ]


def wall_model(sample, theta, phi, height, wall_temp, viscosity):
    sin_theta = jnp.sin(theta)
    normal = [sin_theta * jnp.cos(phi), sin_theta * jnp.sin(phi), jnp.cos(theta)]
    normal_speed = sample[0] * normal[0] + sample[1] * normal[1] + sample[2] * normal[2]
    tangent = [sample[d] - normal_speed * normal[d] for d in range(3)]
    length = jnp.sqrt(tangent[0] * tangent[0] + tangent[1] * tangent[1] + tangent[2] * tangent[2])
    tangent_speed = jnp.maximum(length, speed_floor)
    ladder = (lax.broadcasted_iota(jnp.int32, (NPTS, POINTS), 0).astype(jnp.float32) + 0.5) / NPTS
    heights = height * (ladder * ladder)
    quad_weights = height * (ladder * (2.0 / NPTS))
    rise = karman * heights
    slope_weights = quad_weights * rise
    friction = jnp.sqrt(viscosity * tangent_speed / height)
    for newton_step in range(NEWTON):
        inverse = 1.0 / (viscosity + rise * friction)
        inverse_sum = jnp.sum(quad_weights * inverse, axis=0, keepdims=True)
        slope_sum = jnp.sum(slope_weights * (inverse * inverse), axis=0, keepdims=True)
        residual = friction * friction * inverse_sum - tangent_speed
        derivative = 2.0 * friction * inverse_sum - friction * friction * slope_sum
        friction = friction - residual / derivative
    conduct = viscosity / prandtl + rise * (friction / turb_prandtl)
    resist = jnp.sum(quad_weights / conduct, axis=0, keepdims=True)
    stress = friction * friction / tangent_speed
    return [stress * tangent[0], stress * tangent[1], stress * tangent[2], (sample[3] - wall_temp) / resist]


def walls(owner, received, sampled, flux):
    values = face_values(owner[...], received[...])
    both = jnp.concatenate([sampled[n] for n in range(POINTS // LANES)], axis=1)
    total = both[0:COMPS] + both[COMPS : 2 * COMPS]
    rows = wall_model([total[c : c + 1] for c in range(COMPS)], *values)
    for c in range(COMPS):
        flux[c : c + 1, :] = rows[c]


def run_walls(owner, received, sampled):
    return pl.pallas_call(
        walls,
        out_shape=jax.ShapeDtypeStruct((COMPS, POINTS), jnp.float32),
        in_specs=[vmem_spec] * 3,
        out_specs=vmem_spec,
        name="walls",
    )(owner, on_chip(received), on_chip(sampled))


def on_device(
    state, sample_cell, sample_frac, sample_owner, face_angles, face_height, wall_temp, face_visc
):
    count = lax.axis_size("blk")
    ahead = [(i, (i + 1) % count) for i in range(count)]
    back = [((i + 1) % count, i) for i in range(count)]
    to_west, to_east, packed = run_opening(
        state, face_angles, face_height.reshape(1, -1), wall_temp.reshape(1, -1), face_visc.reshape(1, -1)
    )
    west_halo = lax.ppermute(to_east, "blk", ahead)
    east_halo = lax.ppermute(to_west, "blk", back)
    received = lax.all_to_all(packed, "blk", split_axis=0, concat_axis=0, tiled=True)
    S, M, begun = run_interior(state)
    final, sampled = run_edges(sample_cell, sample_frac, S, M, west_halo, east_halo, begun)
    return final, run_walls(sample_owner.reshape(1, POINTS), received, sampled)


def solution(mesh):
    placed = (
        P(None, "blk", None, None),
        P("blk"),
        P(None, "blk"),
        P("blk", None),
        P(None, "blk"),
        P("blk"),
        P("blk"),
        P("blk"),
    )
    return jax.shard_map(
        on_device,
        mesh=mesh,
        in_specs=placed,
        out_specs=(P(None, "blk", None, None), P(None, "blk")),
        check_vma=False,
    )
```

```python
import functools
import jax
import jax.numpy as jnp
from jax import lax
from jax.experimental import pallas as pl
from jax.experimental.pallas import tpu as pltpu
from jax.sharding import PartitionSpec as P

CX = 16
NY = 128
NZ = 256
POINTS = 512
NPTS = 64
NEWTON = 3
CAP = 8
COMPS = 4
LANES = 128
HALVES = NZ // LANES
PITCH = NY + 8
BLOCKS = HALVES * COMPS
LAYER = BLOCKS * PITCH
TILES = NY // 8
SHEET = BLOCKS * NY

time_step = 0.1
grid_viscosity = 0.2
karman = 0.41
prandtl = 0.72
turb_prandtl = 0.9
speed_floor = 0.5


def load8(flat, base, pitch):
    return [[flat[pl.ds(base + (h * COMPS + c) * pitch, 8), :] for c in range(COMPS)] for h in range(HALVES)]


def load8a(flat, base, pitch):
    return [
        [flat[pl.ds(pl.multiple_of(base + (h * COMPS + c) * pitch, 8), 8), :] for c in range(COMPS)]
        for h in range(HALVES)
    ]


def store8(flat, base, pitch, tiles):
    for h in range(HALVES):
        for c in range(COMPS):
            flat[pl.ds(pl.multiple_of(base + (h * COMPS + c) * pitch, 8), 8), :] = tiles[h][c]


def base_of(layer, yb):
    return layer * LAYER + yb * 8 + 8


def shifted(tiles):
    lane = lax.broadcasted_iota(jnp.int32, (8, LANES), 1)
    upper = [[None] * COMPS for _ in range(HALVES)]
    lower = [[None] * COMPS for _ in range(HALVES)]
    for c in range(COMPS):
        r0 = pltpu.roll(tiles[0][c], LANES - 1, 1)
        r1 = pltpu.roll(tiles[1][c], LANES - 1, 1)
        l0 = pltpu.roll(tiles[0][c], 1, 1)
        l1 = pltpu.roll(tiles[1][c], 1, 1)
        upper[0][c] = jnp.where(lane == LANES - 1, r1, r0)
        upper[1][c] = r1
        lower[0][c] = l0
        lower[1][c] = jnp.where(lane == 0, l0, l1)
    return upper, lower


def coefficients(center, scale):
    lane = lax.broadcasted_iota(jnp.int32, (8, LANES), 1)
    rest = grid_viscosity * scale
    coefs = []
    for h in range(HALVES):
        minus, plus = [], []
        for d in range(3):
            drift = center[h][d] * (0.5 * scale)
            minus.append(rest - drift)
            plus.append(rest + drift)
        coefs.append((minus, plus))
    coefs[1][0][2] = jnp.where(lane == LANES - 1, 0.0, coefs[1][0][2])
    coefs[0][1][2] = jnp.where(lane == 0, 0.0, coefs[0][1][2])
    return coefs


def blend(sides, h, c, coefs):
    minus, plus = coefs[h]
    (east, west), (north, south), (upper, lower) = sides
    xs = minus[0] * east[h][c] + plus[0] * west[h][c]
    ys = minus[1] * north[h][c] + plus[1] * south[h][c]
    zs = minus[2] * upper[h][c] + plus[2] * lower[h][c]
    return (xs + ys) + zs


def middle_tile(s, su, sl, shift_base, x, yb):
    b = base_of(x + 2, yb)
    center = load8a(s, b, PITCH)
    sides = (
        (load8a(s, b + LAYER, PITCH), load8a(s, b - LAYER, PITCH)),
        (load8(s, b + 1, PITCH), load8(s, b - 1, PITCH)),
        (load8a(su, shift_base + yb * 8, NY), load8a(sl, shift_base + yb * 8, NY)),
    )
    coefs = coefficients(center, time_step)
    keep = 1.0 - 6.0 * grid_viscosity * time_step
    return [[blend(sides, h, c, coefs) + keep * center[h][c] for c in range(COMPS)] for h in range(HALVES)]


def final_tile(s, m, mu, ml, shift_base, x, yb, east=None):
    b = base_of(x + 1, yb)
    center = load8a(m, b, PITCH)
    sides = (
        (load8a(m, b + LAYER, PITCH) if east is None else east, load8a(m, b - LAYER, PITCH)),
        (load8(m, b + 1, PITCH), load8(m, b - 1, PITCH)),
        (load8a(mu, shift_base + yb * 8, NY), load8a(ml, shift_base + yb * 8, NY)),
    )
    coefs = coefficients(center, 0.5 * time_step)
    keep = 0.5 - 3.0 * grid_viscosity * time_step
    old = load8a(s, base_of(x + 2, yb), PITCH)
    return [
        [blend(sides, h, c, coefs) + (keep * center[h][c] + 0.5 * old[h][c]) for c in range(COMPS)]
        for h in range(HALVES)
    ]


def shifted_tile(field, layer, yb):
    return shifted(load8a(field, base_of(layer, yb), PITCH))


def store_shifted(u_ref, l_ref, base, pair):
    store8(u_ref, base, NY, pair[0])
    store8(l_ref, base, NY, pair[1])


def zero_pads(ref, layers):
    def body(x, carry):
        for h in range(HALVES):
            for c in range(COMPS):
                ref[x, h, c, 0:8, :] = jnp.zeros((8, LANES), jnp.float32)
        return carry

    lax.fori_loop(0, layers, body, 0)


def half_layer(array, x, h):
    return array.at[:, x, :, pl.ds(h * LANES, LANES)]


S_SHAPE = (CX + 5, HALVES, COMPS, PITCH, LANES)
M_SHAPE = (CX + 3, HALVES, COMPS, PITCH, LANES)
RIM_SHAPE = (COMPS, 2, NY, NZ)
LAG = 3

hbm_spec = pl.BlockSpec(memory_space=pl.ANY)
vmem_spec = pl.BlockSpec(memory_space=pltpu.VMEM)
smem_spec = pl.BlockSpec(memory_space=pltpu.SMEM)
sheet = pltpu.VMEM((SHEET, LANES), jnp.float32)


def in_hbm(x):
    return pltpu.with_memory_space_constraint(x, pltpu.HBM)


def on_chip(x):
    return pltpu.with_memory_space_constraint(x, pltpu.VMEM)


def packed_faces(rows):
    lane = lax.broadcasted_iota(jnp.int32, (LANES, LANES), 1)
    sub = lax.broadcasted_iota(jnp.int32, (LANES, LANES), 0)
    per = LANES // CAP
    mine = lax.shift_right_logical(lane, 3) == (sub & (per - 1))
    left, right = [], []
    for v, row in enumerate(rows):
        spread = jnp.concatenate(
            [jnp.broadcast_to(row[:, q * LANES : (q + 1) * LANES], (per, LANES)) for q in range(CAP)], axis=0
        )
        left.append(jnp.where(mine, spread, 0.0))
        right.append(((sub & (CAP - 1)) + v * CAP == lane).astype(jnp.float32))
    return jnp.dot(
        jnp.concatenate(left, axis=1),
        jnp.concatenate(right, axis=0),
        precision=lax.Precision.HIGHEST,
        preferred_element_type=jnp.float32,
    )


def opening(state, angles, height, temp, visc, to_west, to_east, packed, stage, rim_sem, out_sem):
    def rim_copy(k, c):
        if k == 0:
            return pltpu.make_async_copy(state.at[c, pl.ds(0, 2)], to_west.at[c], rim_sem.at[0, c])
        return pltpu.make_async_copy(state.at[c, pl.ds(CX - 2, 2)], stage.at[c], rim_sem.at[1, c])

    def out_copy(c):
        return pltpu.make_async_copy(stage.at[c], to_east.at[c], out_sem.at[c])

    for k in (1, 0):
        for c in range(COMPS):
            rim_copy(k, c).start()
    for c in range(COMPS):
        rim_copy(1, c).wait()
        out_copy(c).start()
    packed[...] = packed_faces([angles[0:1, :], angles[1:2, :], height[...], temp[...], visc[...]])
    for c in range(COMPS):
        rim_copy(0, c).wait()
        out_copy(c).wait()


def run_opening(state, angles, height, temp, visc):
    f32 = jnp.float32
    return pl.pallas_call(
        opening,
        out_shape=(
            pltpu.VMEM(RIM_SHAPE, f32),
            jax.ShapeDtypeStruct(RIM_SHAPE, f32),
            jax.ShapeDtypeStruct((LANES, LANES), f32),
        ),
        in_specs=[hbm_spec, vmem_spec, vmem_spec, vmem_spec, vmem_spec],
        out_specs=(vmem_spec, hbm_spec, vmem_spec),
        scratch_shapes=[
            pltpu.VMEM(RIM_SHAPE, f32),
            pltpu.SemaphoreType.DMA((2, COMPS)),
            pltpu.SemaphoreType.DMA((COMPS,)),
        ],
        name="opening",
    )(in_hbm(state), angles, height, temp, visc)


def interior(state, S, M, final, F, SU, SL, MU, ML, in_sem, out_sem):
    def in_copy(x, h):
        return pltpu.make_async_copy(half_layer(state, x, h), S.at[x + 2, h, :, pl.ds(8, NY), :], in_sem.at[x, h])

    def out_copy(y, h):
        return pltpu.make_async_copy(F.at[y - 2, h], half_layer(final, y, h), out_sem.at[y - 2, h])

    for x in range(CX):
        for h in range(HALVES):
            in_copy(x, h).start()
    zero_pads(S, CX + 5)
    zero_pads(M, CX + 3)
    s = S.reshape((CX + 5) * LAYER, LANES)
    m = M.reshape((CX + 3) * LAYER, LANES)
    f = F.reshape((CX - 4) * SHEET, LANES)
    def landed(x):
        for h in range(HALVES):
            in_copy(x, h).wait()

    landed(0)
    landed(1)
    for yb in range(TILES):
        store_shifted(SU, SL, yb * 8, shifted_tile(s, 3, yb))

    def sweep(x, with_final):
        landed(x + 1)
        mids = [middle_tile(s, SU, SL, 0, x, yb) for yb in range(TILES)]
        if with_final:
            rb = ((x - 1) & 1) * SHEET
            fins = [final_tile(s, m, MU, ML, rb, x - 1, yb, mids[yb]) for yb in range(TILES)]
        news = [shifted_tile(s, x + 3, yb) for yb in range(TILES)]
        for yb in range(TILES):
            store8(m, base_of(x + 1, yb), PITCH, mids[yb])
            if with_final:
                store8(f, (x - 3) * SHEET + yb * 8, NY, fins[yb])
            store_shifted(SU, SL, yb * 8, news[yb])
            store_shifted(MU, ML, (x & 1) * SHEET + yb * 8, shifted(mids[yb]))
        if with_final:
            for h in range(HALVES):
                out_copy(x - 1, h).start()

    def head(x, carry):
        sweep(x, False)
        return carry

    def main(x, carry):
        sweep(x, True)
        return carry

    lax.fori_loop(1, 3, head, 0)
    lax.fori_loop(3, CX - 1, main, 0)
    for y in range(2, CX - 2):
        for h in range(HALVES):
            out_copy(y, h).wait()


def run_interior(state):
    f32 = jnp.float32
    return pl.pallas_call(
        interior,
        out_shape=(
            pltpu.VMEM(S_SHAPE, f32),
            pltpu.VMEM(M_SHAPE, f32),
            jax.ShapeDtypeStruct((COMPS, CX, NY, NZ), f32),
        ),
        in_specs=[hbm_spec],
        out_specs=(vmem_spec, vmem_spec, hbm_spec),
        scratch_shapes=[pltpu.VMEM((CX - 4, HALVES, COMPS, NY, LANES), f32), sheet, sheet]
        + [pltpu.VMEM((2 * SHEET, LANES), f32)] * 2
        + [pltpu.SemaphoreType.DMA((CX, 2)), pltpu.SemaphoreType.DMA((CX - 4, 2))],
        compiler_params=pltpu.CompilerParams(vmem_limit_bytes=14 << 20),
        name="interior",
    )(in_hbm(state))


def edges(
    cells, fracs, S_in, M_in, west_halo, east_halo, begun, S, M, final, sampled,
    F, SU0, SL0, SU1, SL1, MU, ML, in_sem, out_sem,
):
    def in_copy(k, h):
        array = west_halo if k < 2 else east_halo
        layer = k if k < 2 else CX + k
        return pltpu.make_async_copy(
            half_layer(array, k & 1, h), S.at[layer, h, :, pl.ds(8, NY), :], in_sem.at[k, h]
        )

    for k in range(4):
        for h in range(HALVES):
            in_copy(k, h).start()
    s = S.reshape((CX + 5) * LAYER, LANES)
    m = M.reshape((CX + 3) * LAYER, LANES)
    f = F.reshape(4 * SHEET, LANES)
    rolled = ((SU0, SL0), (SU1, SL1))

    def put_middle(su, sl, x, yb):
        store8(m, base_of(x + 1, yb), PITCH, middle_tile(s, su, sl, 0, x, yb))

    def put_shifted(field, layer, yb, u_ref, l_ref):
        store_shifted(u_ref, l_ref, yb * 8, shifted_tile(field, layer, yb))

    def mid_refs(n):
        return MU.at[pl.ds(n * SHEET, SHEET)], ML.at[pl.ds(n * SHEET, SHEET)]

    for yb in range(TILES):
        put_shifted(s, 2, yb, *rolled[0])
        put_shifted(m, 2, yb, *mid_refs(1))
    for k in range(4):
        for h in range(HALVES):
            in_copy(k, h).wait()
    for yb in range(TILES):
        put_middle(*rolled[0], 0, yb)
        put_shifted(s, CX + 1, yb, *rolled[1])
        put_shifted(m, CX - 1, yb, *mid_refs(2))
    for yb in range(TILES):
        put_middle(*rolled[1], CX - 1, yb)
        put_shifted(s, 1, yb, *rolled[0])
        put_shifted(m, 1, yb, *mid_refs(0))
    for yb in range(TILES):
        put_middle(*rolled[0], -1, yb)
        put_shifted(s, CX + 2, yb, *rolled[1])
        put_shifted(m, CX, yb, *mid_refs(3))
    for yb in range(TILES):
        put_middle(*rolled[1], CX, yb)

    def final_layer(n):
        return (n & 1) + (n >> 1) * (CX - 2)

    def out_copy(n, h):
        return pltpu.make_async_copy(F.at[n, h], half_layer(final, final_layer(n), h), out_sem.at[n, h])

    lane = lax.broadcasted_iota(jnp.int32, (8, LANES), 1)
    along = lane + LANES * (lax.broadcasted_iota(jnp.int32, (8, LANES), 0) // COMPS)

    def sampled_at(e):
        cell = cells[e]
        row = (lax.shift_right_logical(cell, 15) + 1) * LAYER + 8 + (lax.shift_right_logical(cell, 8) & (NY - 1))
        k = cell & (NZ - 1)
        fx, fy, fz = fracs[0, e], fracs[1, e], fracs[2, e]
        near0 = m[pl.ds(row, 8, stride=PITCH), :]
        near1 = m[pl.ds(row + 1, 8, stride=PITCH), :]
        far0 = m[pl.ds(row + LAYER, 8, stride=PITCH), :]
        far1 = m[pl.ds(row + LAYER + 1, 8, stride=PITCH), :]
        wide = (1.0 - fx) * ((1.0 - fy) * near0 + fy * near1) + fx * ((1.0 - fy) * far0 + fy * far1)
        depth = jnp.where(along == k, 1.0 - fz, jnp.where(along == k + 1, fz, 0.0))
        return jnp.sum(wide * depth, axis=1, keepdims=True)

    def last(n, carry):
        total = jnp.zeros((8, LANES), jnp.float32)
        per = LANES // TILES
        for yb in range(TILES):
            tile = final_tile(s, m, MU, ML, n * SHEET, final_layer(n), yb)
            store8(f, n * SHEET + yb * 8, NY, tile)
            for p in range(yb * per, yb * per + per):
                total = jnp.where(lane == p, sampled_at(n * LANES + p), total)
        sampled[n] = total
        for h in range(HALVES):
            out_copy(n, h).start()
        return carry

    lax.fori_loop(0, 4, last, 0)
    for n in range(4):
        for h in range(HALVES):
            out_copy(n, h).wait()


def run_edges(cells, fracs, S, M, west_halo, east_halo, begun):
    f32 = jnp.float32
    outs = pl.pallas_call(
        edges,
        out_shape=(
            pltpu.VMEM(S_SHAPE, f32),
            pltpu.VMEM(M_SHAPE, f32),
            jax.ShapeDtypeStruct((COMPS, CX, NY, NZ), f32),
            pltpu.VMEM((POINTS // LANES, 8, LANES), f32),
        ),
        in_specs=[smem_spec, smem_spec, vmem_spec, vmem_spec, vmem_spec, vmem_spec, hbm_spec],
        out_specs=(vmem_spec, vmem_spec, hbm_spec, vmem_spec),
        input_output_aliases={2: 0, 3: 1, 6: 2},
        scratch_shapes=[pltpu.VMEM((4, HALVES, COMPS, NY, LANES), f32)]
        + [sheet] * 4
        + [
            pltpu.VMEM((4 * SHEET, LANES), f32),
            pltpu.VMEM((4 * SHEET, LANES), f32),
            pltpu.SemaphoreType.DMA((4, 2)),
            pltpu.SemaphoreType.DMA((4, 2)),
        ],
        compiler_params=pltpu.CompilerParams(vmem_limit_bytes=14 << 20),
        name="edges",
    )(cells, fracs, on_chip(S), on_chip(M), on_chip(west_halo), on_chip(east_halo), begun)
    return outs[2], outs[3]


def face_values(owner_row, received):
    owners = lax.broadcasted_iota(jnp.int32, (LANES, POINTS), 0)
    hit = owners == owner_row
    before = lax.broadcasted_iota(jnp.int32, (POINTS, POINTS), 0) < lax.broadcasted_iota(
        jnp.int32, (POINTS, POINTS), 1
    )
    earlier = jnp.dot(
        hit.astype(jnp.bfloat16), before.astype(jnp.bfloat16), preferred_element_type=jnp.float32
    )
    rank = jnp.sum(jnp.where(hit, earlier, 0.0), axis=0, keepdims=True)
    picked = jnp.dot(
        jnp.transpose(received),
        hit.astype(jnp.float32),
        precision=lax.Precision.HIGHEST,
        preferred_element_type=jnp.float32,
    )
    slot = lax.broadcasted_iota(jnp.int32, (CAP, POINTS), 0).astype(jnp.float32) == rank
    return [
        jnp.sum(jnp.where(slot, picked[CAP * v : CAP * v + CAP], 0.0), axis=0, keepdims=True) for v in range(5)
    ]


def wall_model(sample, theta, phi, height, wall_temp, viscosity):
    sin_theta = jnp.sin(theta)
    normal = [sin_theta * jnp.cos(phi), sin_theta * jnp.sin(phi), jnp.cos(theta)]
    normal_speed = sample[0] * normal[0] + sample[1] * normal[1] + sample[2] * normal[2]
    tangent = [sample[d] - normal_speed * normal[d] for d in range(3)]
    length = jnp.sqrt(tangent[0] * tangent[0] + tangent[1] * tangent[1] + tangent[2] * tangent[2])
    tangent_speed = jnp.maximum(length, speed_floor)
    ladder = (lax.broadcasted_iota(jnp.int32, (NPTS, POINTS), 0).astype(jnp.float32) + 0.5) / NPTS
    heights = height * (ladder * ladder)
    quad_weights = height * (ladder * (2.0 / NPTS))
    rise = karman * heights
    slope_weights = quad_weights * rise
    friction = jnp.sqrt(viscosity * tangent_speed / height)
    for newton_step in range(NEWTON):
        inverse = 1.0 / (viscosity + rise * friction)
        inverse_sum = jnp.sum(quad_weights * inverse, axis=0, keepdims=True)
        slope_sum = jnp.sum(slope_weights * (inverse * inverse), axis=0, keepdims=True)
        residual = friction * friction * inverse_sum - tangent_speed
        derivative = 2.0 * friction * inverse_sum - friction * friction * slope_sum
        friction = friction - residual / derivative
    conduct = viscosity / prandtl + rise * (friction / turb_prandtl)
    resist = jnp.sum(quad_weights / conduct, axis=0, keepdims=True)
    stress = friction * friction / tangent_speed
    return [stress * tangent[0], stress * tangent[1], stress * tangent[2], (sample[3] - wall_temp) / resist]


def walls(owner, received, sampled, flux):
    values = face_values(owner[...], received[...])
    both = jnp.concatenate([sampled[n] for n in range(POINTS // LANES)], axis=1)
    total = both[0:COMPS] + both[COMPS : 2 * COMPS]
    rows = wall_model([total[c : c + 1] for c in range(COMPS)], *values)
    for c in range(COMPS):
        flux[c : c + 1, :] = rows[c]


def run_walls(owner, received, sampled):
    return pl.pallas_call(
        walls,
        out_shape=jax.ShapeDtypeStruct((COMPS, POINTS), jnp.float32),
        in_specs=[vmem_spec] * 3,
        out_specs=vmem_spec,
        name="walls",
    )(owner, on_chip(received), on_chip(sampled))


def on_device(
    state, sample_cell, sample_frac, sample_owner, face_angles, face_height, wall_temp, face_visc
):
    count = lax.axis_size("blk")
    ahead = [(i, (i + 1) % count) for i in range(count)]
    back = [((i + 1) % count, i) for i in range(count)]
    to_west, to_east, packed = run_opening(
        state, face_angles, face_height.reshape(1, -1), wall_temp.reshape(1, -1), face_visc.reshape(1, -1)
    )
    west_halo = lax.ppermute(to_east, "blk", ahead)
    east_halo = lax.ppermute(to_west, "blk", back)
    received = lax.all_to_all(packed, "blk", split_axis=0, concat_axis=0, tiled=True)
    S, M, begun = run_interior(state)
    final, sampled = run_edges(sample_cell, sample_frac, S, M, west_halo, east_halo, begun)
    return final, run_walls(sample_owner.reshape(1, POINTS), received, sampled)


def solution(mesh):
    placed = (
        P(None, "blk", None, None),
        P("blk"),
        P(None, "blk"),
        P("blk", None),
        P(None, "blk"),
        P("blk"),
        P("blk"),
        P("blk"),
    )
    return jax.shard_map(
        on_device,
        mesh=mesh,
        in_specs=placed,
        out_specs=(P(None, "blk", None, None), P(None, "blk")),
        check_vma=False,
    )
```
